32 devices in a mesh: aa: 4 (over z), ba: 8 (over y, x, core).
Axes of the slice: x: 2, y: 2, z: 4, core: 2. Of those that a mesh axis runs over, the one named last changes fastest.
Arguments:
- atom_cond: float32 [12288, 128], P(('aa', 'ba')), may hold values from -6 to 6
- noisy_pos: float32 [3, 12288], P(None, ('aa', 'ba')), may hold values from -8 to 8
- noise_level: float32 [1], replicated, may hold values from 0.1 to 4
- atom_token: int32 [12288], P(('aa', 'ba')), may hold values from -1 to 1023, as said below
- token_cond: float32 [1024, 768], P('aa'), may hold values from -6 to 6
- pair: bfloat16 [1024, 1024, 128], P('aa', 'ba'), may hold values from -64 to 64
- pair_bias_weight: bfloat16 [16, 128], replicated, may hold values from -0.375 to 0.375
- gains: float32 [3, 768], replicated, may hold values from 0.25 to 1.75
- w_pos: float32 [3, 128], replicated, may hold values from -3.5 to 3.5
- w_atom_token: bfloat16 [128, 768], replicated, may hold values from -0.5 to 0.5
- w_query_gate: bfloat16 [768, 1536], replicated, may hold values from -0.21875 to 0.21875
- w_key_value: bfloat16 [768, 1536], replicated, may hold values from -0.21875 to 0.21875
- w_attn_out: bfloat16 [768, 768], replicated, may hold values from -0.21875 to 0.21875
- w_up: bfloat16 [768, 3072], replicated, may hold values from -0.21875 to 0.21875
- w_down: bfloat16 [1536, 768], replicated, may hold values from -0.15625 to 0.15625
- w_token_atom: bfloat16 [768, 128], replicated, may hold values from -0.21875 to 0.21875
- w_pos_out: bfloat16 [3, 128], replicated, may hold values from -0.5 to 0.5
Outputs:
- denoised: float32 [3, 12288], P(None, ('aa', 'ba'))
- token_out: float32 [1024, 768], P('aa')
The draws below stay inside these ranges and needn't reach their ends.
Inputs may be any that keep to these rules, and one draw needn't show every extreme that they name: `atom_token`: atom slots come in 4 groups of 3072 consecutive slots; group r holds only atoms of tokens r * 256 to (r + 1) * 256 - 1, in nondecreasing token order, live slots first and -1 after them. Every token has 1 to 12 atoms, and some token of every group has exactly 12.
All inputs are finite; a program needn't handle non-finite values.
Results may differ from the reference program's by a relative error of at most 0.01.
Values may be sent and summed in bfloat16 or wider, within the bound.
A program may use at most 128 MiB of HBM per device.

```python
import math
import jax
import jax.numpy as jnp
from jax import lax

D = 768
HEADS = 16
PAIR_C = 128
ATOM_C = 128
FF = 1536
TOK_A = 256
PER_TOKEN = 12
TOKENS = 1024
ATOMS = 12288
N_BA = 8


def bias_table(key):
    return 0.125 * jax.random.truncated_normal(jax.random.fold_in(key, 11), -3.0, 3.0, (HEADS, PAIR_C), jnp.float32)


def draw_pair_bias_weight(key, part):
    return bias_table(key).astype(jnp.bfloat16)


def draw_pair(key, part):
    base_key = jax.random.fold_in(key, 12)
    field = jax.random.truncated_normal(base_key, -6.0, 6.0, (TOKENS, TOKENS, PAIR_C), jnp.float32)
    table = bias_table(key).astype(jnp.bfloat16).astype(jnp.float32)
    pick_rows = jax.random.randint(jax.random.fold_in(key, 13), (HEADS, 3), 0, TOKENS)
    pick_cols = jax.random.randint(jax.random.fold_in(key, 14), (HEADS, 3), 0, TOKENS)
    pick_steps = jax.random.randint(jax.random.fold_in(key, 15), (HEADS, 3), 1, TOKENS)
    for head_index in range(HEADS):
        sign_row = jnp.sign(table[head_index])
        weight_total = jnp.maximum(jnp.sum(jnp.abs(table[head_index])), 0.5)
        for level_index, strength in enumerate((120.0, 180.0, 240.0)):
            row_pick = pick_rows[head_index, level_index]
            first_col = pick_cols[head_index, level_index]
            second_col = (first_col + pick_steps[head_index, level_index]) % TOKENS
            field = field.at[row_pick, first_col].set(strength / weight_total * sign_row)
            field = field.at[row_pick, second_col].set((strength - 2.0) / weight_total * sign_row)
    return field.astype(jnp.bfloat16)


def draw_atom_token(key, part):
    groups = TOKENS // TOK_A
    upper_count = jax.random.randint(jax.random.fold_in(key, 21), (groups, 1), PER_TOKEN // 2, PER_TOKEN + 1)
    raw_bits = jax.random.randint(jax.random.fold_in(key, 22), (groups, TOK_A), 0, 1 << 20)
    counts = 1 + raw_bits % upper_count
    chosen = jax.random.randint(jax.random.fold_in(key, 23), (groups, 1), 0, TOK_A)
    counts = jnp.where(jnp.arange(TOK_A, dtype=jnp.int32)[None, :] == chosen, PER_TOKEN, counts)
    ends = jnp.cumsum(counts, axis=1)
    slots = jnp.arange(PER_TOKEN * TOK_A, dtype=jnp.int32)
    owner = jnp.sum((ends[:, None, :] <= slots[None, :, None]).astype(jnp.int32), axis=2)
    token_ids = owner + (jnp.arange(groups, dtype=jnp.int32) * TOK_A)[:, None]
    return jnp.where(owner < TOK_A, token_ids, -1).reshape(-1).astype(jnp.int32)


def level_of(stream_key, dims, cuts, low, high):
    factor_of = 1.0
    for dim, parts in cuts:
        draws = jax.random.uniform(jax.random.fold_in(jax.random.fold_in(stream_key, 6), dim), (parts,), jnp.float32, low / len(cuts), high / len(cuts))
        factor_of = factor_of * jnp.repeat(jnp.exp(draws), dims[dim] // parts).reshape((-1,) + (1,) * (len(dims) - 1 - dim))
    return factor_of


def centred(stream_key, shape, width, reach, shards=(), held_as=jnp.bfloat16):
    factor_of = level_of(stream_key, shape, shards, -0.22, 0.18) if shards else 1.0
    entries = jax.random.normal(stream_key, shape, jnp.float32) * width * factor_of
    return jnp.minimum(jnp.maximum(entries, -reach), reach).astype(held_as)


def setup_inputs(seed: int = 0) -> dict:
    streams_of = jax.random.split(jax.random.key(seed), 18)
    return {
        "atom_cond": centred(streams_of[0], (ATOMS, ATOM_C), 1.0, 6.0, ((0, 32),), jnp.float32),
        "noisy_pos": centred(streams_of[1], (3, ATOMS), 1.5, 8.0, ((1, 32),), jnp.float32),
        "noise_level": jnp.clip(jnp.exp(jax.random.uniform(streams_of[2], (1,), jnp.float32, math.log(0.1), math.log(4.0))), 0.1, 4.0),
        "atom_token": draw_atom_token(jax.random.fold_in(streams_of[17], 71), 0),
        "token_cond": centred(streams_of[4], (TOKENS, D), 1.0, 6.0, ((0, 4),), jnp.float32),
        "pair": draw_pair(jax.random.fold_in(streams_of[17], 71), 0),
        "pair_bias_weight": draw_pair_bias_weight(jax.random.fold_in(streams_of[17], 71), 0),
        "gains": jnp.clip(1.0 + 0.15 * jax.random.normal(streams_of[7], (3, D), jnp.float32), 0.25, 1.75),
        "w_pos": centred(streams_of[8], (3, ATOM_C), 3 ** -0.5, 3.5, (), jnp.float32),
        "w_atom_token": centred(streams_of[9], (ATOM_C, D), ATOM_C ** -0.5, 0.5),
        "w_query_gate": centred(streams_of[10], (D, 2 * D), D ** -0.5, 0.21875),
        "w_key_value": centred(streams_of[11], (D, 2 * D), D ** -0.5, 0.21875),
        "w_attn_out": centred(streams_of[12], (D, D), D ** -0.5, 0.21875),
        "w_up": centred(streams_of[13], (D, 2 * FF), D ** -0.5, 0.21875),
        "w_down": centred(streams_of[14], (FF, D), FF ** -0.5, 0.15625),
        "w_token_atom": centred(streams_of[15], (D, ATOM_C), D ** -0.5, 0.21875),
        "w_pos_out": centred(streams_of[16], (3, ATOM_C), ATOM_C ** -0.5, 0.5),
    }


def layer_norm(values, gain_row):
    mean_value = lax.optimization_barrier(jnp.mean(values, axis=-1, keepdims=True))
    centered = values - mean_value
    variance = lax.optimization_barrier(jnp.mean(centered * centered, axis=-1, keepdims=True))
    return centered * lax.rsqrt(variance + 1e-05) * gain_row

def reference(atom_cond, noisy_pos, noise_level, atom_token, token_cond, pair, pair_bias_weight, gains, w_pos, w_atom_token, w_query_gate, w_key_value, w_attn_out, w_up, w_down, w_token_atom, w_pos_out):
    noise_sigma = noise_level[0]
    inv_scale = 1.0 / jnp.sqrt(noise_sigma * noise_sigma + 1.0)
    scaled_pos = noisy_pos * inv_scale
    atom_state = atom_cond + scaled_pos[0][:, None] * w_pos[0]
    atom_state = atom_state + scaled_pos[1][:, None] * w_pos[1]
    atom_state = atom_state + scaled_pos[2][:, None] * w_pos[2]
    hidden_atom = jax.nn.relu(jnp.dot(atom_state.astype(jnp.bfloat16), w_atom_token, preferred_element_type=jnp.float32)).astype(jnp.bfloat16)
    live_mask = atom_token >= 0
    segment_ids = jnp.where(live_mask, atom_token, TOKENS).astype(jnp.int32)
    summed = jax.ops.segment_sum(hidden_atom.astype(jnp.float32), segment_ids, num_segments=TOKENS + 1)[:TOKENS]
    counts = jax.ops.segment_sum(live_mask.astype(jnp.float32), segment_ids, num_segments=TOKENS + 1)[:TOKENS]
    tokens_start = token_cond + summed / counts[:, None]
    normed = layer_norm(tokens_start, gains[0]).astype(jnp.bfloat16)
    query_gate = jnp.dot(normed, w_query_gate, preferred_element_type=jnp.float32)
    query_rows = query_gate[:, :D].astype(jnp.bfloat16)
    gate_value = jax.nn.sigmoid(query_gate[:, D:]).astype(jnp.bfloat16)
    key_value = jnp.dot(normed, w_key_value, preferred_element_type=jnp.float32).astype(jnp.bfloat16)
    head_dim = D // HEADS
    block_cols = TOKENS // N_BA
    query_heads = query_rows.astype(jnp.float32).reshape(TOKENS, HEADS, head_dim)
    bias_weight = pair_bias_weight.astype(jnp.float32)

    def one_block(block_index):
        start_row = block_index * block_cols
        kv_block = lax.dynamic_slice_in_dim(key_value, start_row, block_cols, 0).astype(jnp.float32)
        key_heads = kv_block[:, :D].reshape(block_cols, HEADS, head_dim)
        value_heads = kv_block[:, D:].reshape(block_cols, HEADS, head_dim)
        pair_block = lax.dynamic_slice_in_dim(pair, start_row, block_cols, 1).astype(jnp.float32)
        scores = jnp.einsum('ihd,jhd->hij', query_heads, key_heads) * head_dim ** (-0.5) + jnp.einsum('hc,ijc->hij', bias_weight, pair_block)
        block_max = lax.optimization_barrier(jnp.max(scores, axis=2))
        weights = jnp.exp(scores - block_max[:, :, None])
        block_total = lax.optimization_barrier(jnp.sum(weights, axis=2))
        rounded = lax.optimization_barrier(weights.astype(jnp.bfloat16)).astype(jnp.float32)
        partial_out = jnp.einsum('hij,jhd->ihd', rounded, value_heads).reshape(TOKENS, D)
        return (block_max, block_total, partial_out)
    maxima, totals, outputs = lax.map(one_block, jnp.arange(N_BA, dtype=jnp.int32))
    overall = lax.optimization_barrier(jnp.max(maxima, axis=0))
    factors = jnp.exp(maxima - overall[None])
    total_all = lax.optimization_barrier(jnp.sum(factors * totals, axis=0))
    widened = jnp.repeat(jnp.transpose(factors, (0, 2, 1)), head_dim, axis=2)
    out_all = lax.optimization_barrier(jnp.sum(widened * outputs, axis=0))
    attended = out_all / jnp.repeat(total_all.T, head_dim, axis=1)
    mixed_heads = (attended * gate_value.astype(jnp.float32)).astype(jnp.bfloat16)
    tokens_mid = tokens_start + jnp.dot(mixed_heads, w_attn_out, preferred_element_type=jnp.float32)
    normed_mid = layer_norm(tokens_mid, gains[1]).astype(jnp.bfloat16)
    gate_up = jnp.dot(normed_mid, w_up, preferred_element_type=jnp.float32)
    inner_units = (jax.nn.silu(gate_up[:, :FF]) * gate_up[:, FF:]).astype(jnp.bfloat16)
    token_out = tokens_mid + jnp.dot(inner_units, w_down, preferred_element_type=jnp.float32)
    normed_out = layer_norm(token_out, gains[2]).astype(jnp.bfloat16)
    token_atom = jnp.dot(normed_out, w_token_atom, preferred_element_type=jnp.float32).astype(jnp.bfloat16)
    safe_ids = jnp.clip(atom_token, 0, TOKENS - 1).astype(jnp.int32)
    picked = jnp.where(live_mask[:, None], token_atom[safe_ids].astype(jnp.float32), 0.0)
    atom_final = atom_state + picked
    atom_normed = layer_norm(atom_final, 1.0).astype(jnp.bfloat16)
    update = lax.dot_general(w_pos_out, atom_normed, (((1,), (1,)), ((), ())), preferred_element_type=jnp.float32)
    denoised = noisy_pos * (inv_scale * inv_scale) + update * (noise_sigma * inv_scale)
    return (denoised, token_out)
```

```python
import functools

import jax
import jax.numpy as jnp
from jax import lax
from jax.experimental import pallas as pl
from jax.experimental.pallas import tpu as pltpu
from jax.sharding import PartitionSpec as P

D = 768
HEADS = 16
MESH = pl.DeviceIdType.MESH


def exchange(arrays, axis, n, scatter, collective_id):
    count = len(arrays)

    def kernel(*refs):
        ins, outs = refs[:count], refs[count : 2 * count]
        local_sem, send_sem, recv_sem = refs[2 * count :]
        me = lax.axis_index(axis)
        barrier = pltpu.get_barrier_semaphore()
        for k in range(1, n):
            pl.semaphore_signal(
                barrier, inc=1, device_id={axis: lax.rem(me + k, n)}, device_id_type=MESH
            )
        own = []
        for a in range(count):
            src = ins[a].at[me] if scatter else ins[a]
            own.append(pltpu.make_async_copy(src, outs[a].at[me], local_sem.at[a]))
            own[-1].start()
        pl.semaphore_wait(barrier, n - 1)
        copies = []
        for k in range(1, n):
            peer = lax.rem(me + k, n)
            for a in range(count):
                copy = pltpu.make_async_remote_copy(
                    src_ref=ins[a].at[peer] if scatter else ins[a],
                    dst_ref=outs[a].at[me],
                    send_sem=send_sem.at[a, k - 1],
                    recv_sem=recv_sem.at[a, k - 1],
                    device_id={axis: peer},
                    device_id_type=MESH,
                )
                copy.start()
                copies.append(copy)
        for copy in own + copies:
            copy.wait()

    shapes = [x.shape if scatter else (n, *x.shape) for x in arrays]
    return pl.pallas_call(
        kernel,
        out_shape=[jax.ShapeDtypeStruct(s, x.dtype) for s, x in zip(shapes, arrays)],
        in_specs=[pl.BlockSpec(memory_space=pl.ANY)] * count,
        out_specs=[pl.BlockSpec(memory_space=pl.ANY)] * count,
        scratch_shapes=[
            pltpu.SemaphoreType.DMA((count,)),
            pltpu.SemaphoreType.DMA((count, n - 1)),
            pltpu.SemaphoreType.DMA((count, n - 1)),
        ],
        compiler_params=pltpu.CompilerParams(collective_id=collective_id, has_side_effects=True),
    )(*arrays)


def spread(rows, n, per_row, offset_of, collective_id):
    def kernel(in_ref, out_ref, local_sem, send_sem, recv_sem):
        me = lax.axis_index("aa")
        owner = lax.axis_index("ba") * offset_of // per_row
        barrier = pltpu.get_barrier_semaphore()
        for k in range(1, n):
            pl.semaphore_signal(
                barrier, inc=1, device_id={"aa": lax.rem(me + k, n)}, device_id_type=MESH
            )
        pl.semaphore_wait(barrier, n - 1)

        def copy_to(k):
            return pltpu.make_async_remote_copy(
                src_ref=in_ref,
                dst_ref=out_ref,
                send_sem=send_sem.at[k - 1],
                recv_sem=recv_sem,
                device_id={"aa": lax.rem(me + k, n)},
                device_id_type=MESH,
            )

        @pl.when(me == owner)
        def _():
            for k in range(1, n):
                copy_to(k).start()
            own = pltpu.make_async_copy(in_ref, out_ref, local_sem)
            own.start()
            own.wait()
            for k in range(1, n):
                copy_to(k).wait_send()

        @pl.when(me != owner)
        def _():
            copy_to(1).wait_recv()

    return pl.pallas_call(
        kernel,
        out_shape=jax.ShapeDtypeStruct(rows.shape, rows.dtype),
        in_specs=[pl.BlockSpec(memory_space=pl.ANY)],
        out_specs=pl.BlockSpec(memory_space=pl.ANY),
        scratch_shapes=[
            pltpu.SemaphoreType.DMA,
            pltpu.SemaphoreType.DMA((n - 1,)),
            pltpu.SemaphoreType.DMA,
        ],
        compiler_params=pltpu.CompilerParams(collective_id=collective_id, has_side_effects=True),
    )(rows)


def layer_norm(values, gain_row):
    mean_value = jnp.mean(values, axis=-1, keepdims=True)
    centered = values - mean_value
    variance = jnp.mean(centered * centered, axis=-1, keepdims=True)
    return centered * lax.rsqrt(variance + 1e-05) * gain_row


def token_sums(local_ids, rounded_state, w_atom_token, tok_rows):
    selector = (jnp.arange(tok_rows, dtype=jnp.int32)[:, None] == local_ids[None, :]).astype(
        jnp.bfloat16
    )
    hidden_atom = jax.nn.relu(
        jnp.dot(rounded_state, w_atom_token, preferred_element_type=jnp.float32)
    ).astype(jnp.bfloat16)
    sums = lax.dot_general(
        selector, hidden_atom, (((1,), (0,)), ((), ())), preferred_element_type=jnp.float32
    )
    return (sums, jnp.sum(selector.astype(jnp.float32), axis=1))


def project_start(tokens_start, gains, w_query_gate):
    normed = layer_norm(tokens_start, gains[0]).astype(jnp.bfloat16)
    query_gate = jnp.dot(normed, w_query_gate, preferred_element_type=jnp.float32)
    width = query_gate.shape[1] // 2
    query_rows = query_gate[:, :width].astype(jnp.bfloat16)
    gate_value = jax.nn.sigmoid(query_gate[:, width:]).astype(jnp.bfloat16)
    return (normed, query_rows, gate_value)


def on_device(
    n_aa,
    n_ba,
    atom_cond,
    noisy_pos,
    noise_level,
    atom_token,
    token_cond,
    pair,
    pair_bias_weight,
    gains,
    w_pos,
    w_atom_token,
    w_query_gate,
    w_key_value,
    w_attn_out,
    w_up,
    w_down,
    w_token_atom,
    w_pos_out,
):
    tok_rows = token_cond.shape[0]
    block_cols = pair.shape[1]
    head_dim = D // HEADS
    row_index = lax.axis_index("aa")
    col_index = lax.axis_index("ba")
    noise_sigma = noise_level[0]
    inv_scale = 1.0 / jnp.sqrt(noise_sigma * noise_sigma + 1.0)
    scaled_pos = noisy_pos * inv_scale
    atom_state = atom_cond + scaled_pos[0][:, None] * w_pos[0]
    atom_state = atom_state + scaled_pos[1][:, None] * w_pos[1]
    atom_state = atom_state + scaled_pos[2][:, None] * w_pos[2]
    rounded_state = atom_state.astype(jnp.bfloat16)
    local_token = atom_token - row_index * tok_rows
    one_hot = (local_token[:, None] == jnp.arange(tok_rows, dtype=jnp.int32)[None, :]).astype(
        jnp.bfloat16
    )
    group_state, group_ids = exchange(
        [rounded_state, local_token.reshape(1, -1)], "ba", n_ba, False, 0
    )
    group_state = group_state.reshape(-1, group_state.shape[-1])
    summed, counts = token_sums(
        group_ids.reshape(-1), group_state, w_atom_token, tok_rows
    )
    tokens_start = token_cond + summed / counts[:, None]
    normed, query_rows, gate_value = project_start(tokens_start, gains, w_query_gate)
    offset_row = col_index * block_cols % tok_rows
    slice_rows = lax.dynamic_slice_in_dim(normed, offset_row, block_cols, 0)
    block_rows = spread(slice_rows, n_aa, tok_rows, block_cols, 1)
    key_value = jnp.dot(block_rows, w_key_value, preferred_element_type=jnp.float32).astype(
        jnp.bfloat16
    )
    key_heads = key_value[:, :D].reshape(block_cols, HEADS, head_dim)
    value_heads = key_value[:, D:].reshape(block_cols, HEADS, head_dim)
    query_heads = query_rows.reshape(tok_rows, HEADS, head_dim)
    scores = jnp.einsum(
        "ihd,jhd->hij", query_heads, key_heads, preferred_element_type=jnp.float32
    ) * head_dim ** (-0.5) + jnp.einsum(
        "hc,ijc->hij", pair_bias_weight, pair, preferred_element_type=jnp.float32
    )
    block_max = jnp.max(scores, axis=2)
    weights = jnp.exp(scores - block_max[:, :, None])
    block_total = jnp.sum(weights, axis=2)
    partial_out = jnp.einsum(
        "hij,jhd->ihd",
        weights.astype(jnp.bfloat16),
        value_heads,
        preferred_element_type=jnp.float32,
    ).reshape(tok_rows, D)
    own_rows = tok_rows // n_ba
    stats = jnp.concatenate([block_max, block_total], axis=0).T
    out_all, stats_all = exchange(
        [
            partial_out.astype(jnp.bfloat16).reshape(n_ba, own_rows, D),
            stats.reshape(n_ba, own_rows, 2 * HEADS),
        ],
        "ba",
        n_ba,
        True,
        2,
    )
    max_all, total_all = stats_all[:, :, :HEADS], stats_all[:, :, HEADS:]
    factor = jnp.exp(max_all - jnp.max(max_all, axis=0, keepdims=True))
    share = factor / jnp.sum(factor * total_all, axis=0, keepdims=True)
    wide_share = jnp.repeat(share, head_dim, axis=2)
    attended = jnp.sum(wide_share * out_all.astype(jnp.float32), axis=0)
    gate_rows = lax.dynamic_slice_in_dim(gate_value, col_index * own_rows, own_rows, 0)
    mixed_rows = (attended * gate_rows.astype(jnp.float32)).astype(jnp.bfloat16)
    mixed_heads = exchange([mixed_rows], "ba", n_ba, False, 3)[0].reshape(tok_rows, D)
    tokens_mid = tokens_start + jnp.dot(mixed_heads, w_attn_out, preferred_element_type=jnp.float32)
    normed_mid = layer_norm(tokens_mid, gains[1]).astype(jnp.bfloat16)
    gate_up = jnp.dot(normed_mid, w_up, preferred_element_type=jnp.float32)
    hidden_units = w_down.shape[0]
    inner_units = (jax.nn.silu(gate_up[:, :hidden_units]) * gate_up[:, hidden_units:]).astype(
        jnp.bfloat16
    )
    token_out = tokens_mid + jnp.dot(inner_units, w_down, preferred_element_type=jnp.float32)
    normed_out = layer_norm(token_out, gains[2]).astype(jnp.bfloat16)
    token_atom = jnp.dot(normed_out, w_token_atom, preferred_element_type=jnp.float32).astype(
        jnp.bfloat16
    )
    picked = jnp.dot(one_hot, token_atom, preferred_element_type=jnp.float32)
    atom_final = atom_state + picked
    atom_normed = layer_norm(atom_final, 1.0).astype(jnp.bfloat16)
    update = lax.dot_general(
        w_pos_out, atom_normed, (((1,), (1,)), ((), ())), preferred_element_type=jnp.float32
    )
    denoised = noisy_pos * (inv_scale * inv_scale) + update * (noise_sigma * inv_scale)
    return (denoised, token_out)


def solution(mesh):
    in_specs = (
        P(("aa", "ba"), None),
        P(None, ("aa", "ba")),
        P(),
        P(("aa", "ba")),
        P("aa", None),
        P("aa", "ba", None),
        P(),
        P(),
        P(),
        P(),
        P(),
        P(),
        P(),
        P(),
        P(),
        P(),
        P(),
    )
    out_specs = (P(None, ("aa", "ba")), P("aa", None))
    return jax.shard_map(
        functools.partial(on_device, mesh.shape["aa"], mesh.shape["ba"]),
        mesh=mesh, in_specs=in_specs, out_specs=out_specs, check_vma=False
    )
```
